32 devices in a mesh: grp: 2 (over y), tp: 4 (over z), dp: 2 (over x), sub: 2 (over core).
Axes of the slice: x: 2, y: 2, z: 4, core: 2. Of those that a mesh axis runs over, the one named last changes fastest.
Arguments:
- hidden_in: bfloat16 [240, 26624], P(('grp', 'dp', 'sub'), 'tp'), parts along dimension 0, may hold values from -6 to 6
- out_grad: bfloat16 [240, 8192], P(('grp', 'tp'), ('dp', 'sub')), parts along dimension 0, may hold values from -6 to 6
- base_levels: bfloat16 [26624, 8192], P('tp', ('dp', 'sub')), may hold values from -1 to 1, as said below
- base_scales: bfloat16 [416, 8192], P('tp', ('dp', 'sub')), may hold values from 0.0079956055 to 0.015991211
- kron_outer: float32 [4, 4], P('tp', ('dp', 'sub')), may hold values from -3 to 3
- kron_left: bfloat16 [6656, 16], replicated, may hold values from -0.078125 to 0.078125
- kron_right: bfloat16 [16, 2048], replicated, may hold values from -0.125 to 0.125
- sparse_rows: int32 [4, 4, 8], P('tp', ('dp', 'sub')), may hold values from 0 to 51, as said below
- sparse_cols: int32 [4, 4, 8], P('tp', ('dp', 'sub')), may hold values from 0 to 15, as said below
- sparse_count: int32 [4, 4], P('tp', ('dp', 'sub')), may hold values from 1 to 8, as said below
- sparse_values: bfloat16 [4, 4, 8, 128, 128], P('tp', ('dp', 'sub')), may hold values from -0.3125 to 0.3125
Outputs:
- layer_out: bfloat16 [240, 8192], P(('grp', 'tp'), ('dp', 'sub')), parts along dimension 0
- input_grad: bfloat16 [240, 26624], P(('grp', 'dp', 'sub'), 'tp'), parts along dimension 0
- grad_outer: float32 [8, 4], P(('grp', 'tp'), ('dp', 'sub')), parts along dimension 0
- grad_left: float32 [13312, 16], P('grp'), parts along dimension 0
- grad_right: float32 [32, 2048], P('grp'), parts along dimension 0
- grad_sparse: float32 [8, 4, 8, 128, 128], P(('grp', 'tp'), ('dp', 'sub')), parts along dimension 0
The draws below stay inside these ranges and needn't reach their ends.
There are 2 independent parts, one for each index of `grp`. The reference program is written for one: setup_inputs(seed, part) draws one part's arguments, and reference() takes and returns one part's arrays. A program takes and returns all parts, laid end to end along the dimension named above; an argument that names none is the same for every part. Nothing has to cross between parts.
Inputs may be any that keep to these rules, and one draw needn't show every extreme that they name: `base_levels`: every entry is one of the 16 levels of the NF4 code. `sparse_rows`: the 8 slots of a tile name distinct blocks, with sparse_cols. `sparse_cols`: the 8 slots of a tile name distinct blocks, with sparse_rows. `sparse_count`: slots at or past the count are unused; some tile uses all 8.
All inputs are finite; a program needn't handle non-finite values.
Results may differ from the reference program's by a relative error of at most 0.014.
Values may be sent and summed in bfloat16 or wider, within the bound.
A program may use at most 320 MiB of HBM per device.

```python
import math
import jax
import jax.numpy as jnp
from jax import lax

K = 26624
D = 8192
R = 16
BLK = 128
QB = 64
MAXB = 8
TOKENS = 120
KRON_ROWS = 4
KRON_COLS = 4
KT = 6656
DS = 2048


NF4_LEVELS = [-1.0, -0.6961928009986877, -0.5250730514526367, -0.39491748809814453, -0.28444138169288635, -0.18477343022823334, -0.09105003625154495, 0.0, 0.07958029955625534, 0.16093020141124725, 0.24611230194568634, 0.33791524171829224, 0.44070982933044434, 0.5626170039176941, 0.7229568362236023, 1.0]


def draw_base_levels(key, part):
    codes = jax.random.randint(key, (K, D), 0, 16)
    table = jnp.array(NF4_LEVELS, dtype=jnp.float32)
    return jnp.take(table, codes).astype(jnp.bfloat16)


def tile_choice(tile_key):
    per_tile = KT // BLK * (DS // BLK)
    return jax.random.permutation(tile_key, per_tile)[:MAXB]


def slot_positions(key):
    tile_total = KRON_ROWS * KRON_COLS
    tile_keys = jax.random.split(jax.random.fold_in(key, 7), tile_total)
    chosen = jax.vmap(tile_choice)(tile_keys)
    return chosen.reshape(KRON_ROWS, KRON_COLS, MAXB).astype(jnp.int32)


def draw_sparse_rows(key, part):
    return (slot_positions(key) // (DS // BLK)).astype(jnp.int32)


def draw_sparse_cols(key, part):
    return (slot_positions(key) % (DS // BLK)).astype(jnp.int32)


def draw_sparse_count(key, part):
    tile_total = KRON_ROWS * KRON_COLS
    counts = jax.random.randint(jax.random.fold_in(key, 11), (tile_total,), 1, MAXB + 1)
    fullest = jax.random.randint(jax.random.fold_in(key, 13), (), 0, tile_total)
    counts = jnp.where(jnp.arange(tile_total) == fullest, MAXB, counts)
    return counts.reshape(KRON_ROWS, KRON_COLS).astype(jnp.int32)


def raised(entries, key, source, target, blocks, factor):
    owner, partner = [(jnp.arange(entries.shape[axis_at]) // (entries.shape[axis_at] // blocks)).reshape([-1 if axis == axis_at else 1 for axis in range(entries.ndim)]) for axis_at in (source, target)]
    chosen = jax.random.permutation(key, blocks)[partner]
    strong = (owner == chosen) | (owner == (partner + blocks // 2) % blocks)
    return jnp.where(strong, factor * entries, entries)


def level_of(rng, extent, cuts, low, top_value):
    gain = 1.0
    for axis_at, blocks in cuts:
        draws = jax.random.uniform(jax.random.fold_in(jax.random.fold_in(rng, 6), axis_at), (blocks,), jnp.float32, low / len(cuts), top_value / len(cuts))
        gain = gain * jnp.repeat(jnp.exp(draws), extent[axis_at] // blocks).reshape((-1,) + (1,) * (len(extent) - 1 - axis_at))
    return gain


def noise(rng, shape, width, most, cuts=(), held_as=jnp.bfloat16):
    factor_of = level_of(rng, shape, cuts, -0.22, 0.18) if cuts else 1.0
    drawn = jax.random.normal(rng, shape, jnp.float32) * width * factor_of
    return jnp.minimum(jnp.maximum(drawn, -most), most).astype(held_as)


def heavy_noise(stream_key, dims, scale, bound, pieces, heavy, kind=jnp.bfloat16):
    result = scale * jax.random.normal(stream_key, dims, jnp.float32)
    if pieces:
        result = result * level_of(stream_key, dims, pieces, -0.22, 0.18)
    return jnp.clip(raised(result, jax.random.fold_in(stream_key, 3), *heavy), -bound, bound).astype(kind)


def setup_inputs(seed: int = 0, part: int = 0) -> dict:
    splits = jax.random.split(jax.random.key(seed), 12)
    part_splits = jax.random.split(jax.random.fold_in(splits[11], part), 12)
    return {
        "hidden_in": heavy_noise(part_splits[0], (TOKENS, K), 1.0, 6.0, ((0, 4), (1, 4)), (1, 0, 4, 2.0)),
        "out_grad": heavy_noise(part_splits[1], (TOKENS, D), 1.0, 6.0, ((0, 4), (1, 4)), (1, 0, 4, 2.0)),
        "base_levels": draw_base_levels(jax.random.fold_in(splits[11], 71), part),
        "base_scales": jnp.clip(jnp.exp(math.log(0.015991211) - 0.6931472 * jax.random.uniform(splits[3], (K // QB, D), jnp.float32) ** level_of(splits[3], (K // QB, D), ((0, 4), (1, 4)), -0.2, 0.2)), 0.0079956055, 0.015991211).astype(jnp.bfloat16),
        "kron_outer": noise(splits[4], (KRON_ROWS, KRON_COLS), 0.6, 3.0, ((0, 4), (1, 4)), jnp.float32),
        "kron_left": noise(splits[5], (KT, R), KT ** -0.5, 0.078125),
        "kron_right": noise(splits[6], (R, DS), DS ** -0.5, 0.125),
        "sparse_rows": draw_sparse_rows(jax.random.fold_in(splits[11], 71), part),
        "sparse_cols": draw_sparse_cols(jax.random.fold_in(splits[11], 71), part),
        "sparse_count": draw_sparse_count(jax.random.fold_in(splits[11], 71), part),
        "sparse_values": noise(splits[10], (KRON_ROWS, KRON_COLS, MAXB, BLK, BLK), 0.02, 0.3125, ((0, 4), (1, 4))),
    }


def block_delta(rows_tile, cols_tile, count_tile, values_tile):
    slot_ids = jnp.arange(MAXB).astype(jnp.int32)
    live_slots = (slot_ids[None, :] < count_tile[:, None]).astype(jnp.float32)
    row_ids = jnp.arange(KT // BLK).astype(jnp.int32)
    col_ids = jnp.arange(DS // BLK).astype(jnp.int32)
    row_onehot = (rows_tile[..., None] == row_ids[None, None, :]).astype(jnp.float32) * live_slots[..., None]
    col_onehot = (cols_tile[..., None] == col_ids[None, None, :]).astype(jnp.float32)
    placed = jnp.einsum("sma,smb,smij->aisbj", row_onehot, col_onehot, values_tile.astype(jnp.float32), precision=lax.Precision.HIGHEST)
    return placed.reshape(KT, KRON_COLS * DS)


def reference(hidden_in, out_grad, base_levels, base_scales, kron_outer, kron_left, kron_right, sparse_rows, sparse_cols, sparse_count, sparse_values):
    highest = lax.Precision.HIGHEST
    grad_split = out_grad.reshape(TOKENS, KRON_COLS, DS)
    grad_proj = jnp.einsum("tsd,rd->str", grad_split.astype(jnp.float32), kron_right.astype(jnp.float32), precision=highest).astype(jnp.bfloat16)
    out_total = jnp.zeros((TOKENS, D), jnp.float32)
    left_grad = jnp.zeros((KT, R), jnp.float32)
    right_grad = jnp.zeros((R, DS), jnp.float32)
    grad_columns = []
    outer_rows = []
    sparse_tiles = []
    slot_ids = jnp.arange(MAXB).astype(jnp.int32)
    for tile_index in range(KRON_ROWS):
        first_row = tile_index * KT
        inputs_tile = hidden_in[:, first_row:first_row + KT]
        levels_tile = base_levels[first_row:first_row + KT].astype(jnp.float32)
        scales_tile = base_scales[first_row // QB:(first_row + KT) // QB].astype(jnp.float32)
        dequant = (levels_tile.reshape(KT // QB, QB, D) * scales_tile[:, None, :]).reshape(KT, D)
        sparse_delta = block_delta(sparse_rows[tile_index], sparse_cols[tile_index], sparse_count[tile_index], sparse_values[tile_index])
        weight = (dequant + sparse_delta).astype(jnp.bfloat16)
        projected = jnp.dot(inputs_tile, kron_left, preferred_element_type=jnp.float32).astype(jnp.bfloat16)
        low_rank = jnp.dot(projected, kron_right, preferred_element_type=jnp.float32)
        outer_row = kron_outer[tile_index]
        kron_part = (outer_row[None, :, None] * low_rank[:, None, :]).reshape(TOKENS, D)
        partial_value = jnp.dot(inputs_tile, weight, preferred_element_type=jnp.float32) + kron_part
        partial_value = lax.optimization_barrier(partial_value.astype(jnp.bfloat16))
        out_total = out_total + partial_value.astype(jnp.float32)
        mixed = jnp.einsum("s,str->tr", outer_row, grad_proj.astype(jnp.float32), precision=highest)
        back = lax.dot_general(out_grad, weight, (((1,), (1,)), ((), ())), preferred_element_type=jnp.float32)
        back = back + jnp.dot(mixed, kron_left.astype(jnp.float32).T, precision=highest)
        grad_columns.append(back.astype(jnp.bfloat16))
        outer_rows.append(jnp.einsum("tr,str->s", projected.astype(jnp.float32), grad_proj.astype(jnp.float32), precision=highest) / TOKENS)
        left_grad = left_grad + jnp.dot(inputs_tile.astype(jnp.float32).T, mixed, precision=highest) / TOKENS
        proj_out = lax.dot_general(projected, out_grad, (((0,), (0,)), ((), ())), preferred_element_type=jnp.float32).reshape(R, KRON_COLS, DS)
        right_grad = right_grad + jnp.einsum("s,rsd->rd", outer_row, proj_out, precision=highest) / TOKENS
        input_blocks = inputs_tile.reshape(TOKENS, KT // BLK, BLK)
        chosen_inputs = jnp.take(input_blocks, sparse_rows[tile_index], axis=1)
        grad_blocks = out_grad.reshape(TOKENS, KRON_COLS, DS // BLK, BLK)
        col_index = jnp.arange(KRON_COLS).astype(jnp.int32)[:, None]
        chosen_grads = grad_blocks[:, col_index, sparse_cols[tile_index], :]
        live_slots = (slot_ids[None, :] < sparse_count[tile_index][:, None]).astype(jnp.float32)
        blocks = jnp.einsum("tsmi,tsmj->smij", chosen_inputs.astype(jnp.float32), chosen_grads.astype(jnp.float32), precision=highest)
        sparse_tiles.append(blocks * live_slots[:, :, None, None] / TOKENS)
    layer_out = out_total.astype(jnp.bfloat16)
    input_grad = jnp.concatenate(grad_columns, axis=1)
    grad_outer = jnp.stack(outer_rows, axis=0)
    grad_sparse = jnp.stack(sparse_tiles, axis=0)
    return (layer_out, input_grad, grad_outer, left_grad, right_grad, grad_sparse)
```

```python
import functools

import jax
import jax.numpy as jnp
from jax import lax
from jax.experimental import pallas as pl
from jax.experimental.pallas import tpu as pltpu
from jax.sharding import PartitionSpec as P

F32 = jnp.float32
BF16 = jnp.bfloat16


def dot(a, b, ca, cb):
    return lax.dot_general(a, b, (((ca,), (cb,)), ((), ())), preferred_element_type=F32)


def pick_rows(tile_rows, tile_cols, block, quant):
    blocks = tile_rows // block
    best = tile_rows
    for n in range(1, blocks):
        if blocks % n == 0 and n * block * tile_cols <= 1 << 20 and n * block % (8 * quant) == 0:
            best = n * block
    return tile_rows if tile_rows * tile_cols <= 1 << 20 else best


def kernel(
    tokens, step_rows,
    slot_ref, rows_ref, cols_ref, count_ref, coef_ref,
    x_ref, dy_ref, kl_ref, kr_ref, sc_ref, val_ref, w_hbm,
    out_ref, ig_ref, go_ref, gl_ref, gr_ref, gs_ref,
    wbuf, wdq, acc, scf, vals, wsem,
):
    tile_rows, tile_cols = w_hbm.shape
    slots, block = val_ref.shape[0], val_ref.shape[1]
    col_blocks = tile_cols // block
    step_blocks = step_rows // block
    steps = tile_rows // step_rows
    quant = tile_rows // sc_ref.shape[0]
    inv = 1.0 / tokens
    coef = coef_ref[0, 0]

    def fetch(i, slot):
        return pltpu.make_async_copy(
            w_hbm.at[pl.ds(i * step_rows, step_rows)], wbuf.at[slot], wsem.at[slot]
        )

    fetch(0, 0).start()
    scf[...] = sc_ref[...].astype(F32)
    vals[pl.ds(0, slots)] = val_ref[...]
    vals[slots] = jnp.zeros((block, block), BF16)

    proj = dot(x_ref[...], kl_ref[...], 1, 0).astype(BF16)
    gproj = dot(dy_ref[...], kr_ref[...], 1, 1).astype(BF16)
    go_ref[...] = (jnp.sum(proj.astype(F32) * gproj.astype(F32)) * inv).reshape(1, 1)
    gl_ref[...] = dot(gproj, x_ref[...], 0, 0) * (coef * inv)
    gr_ref[...] = dot(proj, dy_ref[...], 0, 0) * (coef * inv)
    acc[...] = coef * dot(proj, kr_ref[...], 1, 0)

    @pl.loop(0, slots)
    def _(m):
        xr = x_ref[:, pl.ds(pl.multiple_of(rows_ref[m] * block, block), block)]
        dc = dy_ref[:, pl.ds(pl.multiple_of(cols_ref[m] * block, block), block)]
        live = jnp.where(m < count_ref[0, 0], inv, 0.0)
        gs_ref[m] = dot(xr, dc, 0, 0) * live

    @pl.loop(0, steps)
    def _(i):
        slot = lax.rem(i, 2)

        @pl.when(i + 1 < steps)
        def _():
            fetch(i + 1, 1 - slot).start()

        fetch(i, slot).wait()
        groups = step_rows // quant
        if steps == 1:
            scales = scf[...]
        else:
            scales = scf[pl.ds(pl.multiple_of(i * groups, 8), groups), :]
        for rb in range(step_blocks):
            for cb in range(col_blocks):
                delta = vals[slot_ref[(i * step_blocks + rb) * col_blocks + cb]]
                for q in range(block // quant):
                    r0 = rb * block + q * quant
                    lv = wbuf[slot, r0:r0 + quant, cb * block:(cb + 1) * block]
                    s = scales[r0 // quant:r0 // quant + 1, cb * block:(cb + 1) * block]
                    s16 = jnp.broadcast_to(s, (16, block)).astype(BF16)
                    w = lv.reshape(quant // 16, 16, block) * s16[None]
                    w = w.reshape(quant, block) + delta[q * quant:(q + 1) * quant]
                    wdq[r0:r0 + quant, cb * block:(cb + 1) * block] = w
        cols = pl.ds(pl.multiple_of(i * step_rows, block), step_rows)
        acc[...] += dot(x_ref[:, cols], wdq[...], 1, 0)
        back = dot(dy_ref[...], wdq[...], 1, 1)
        back += coef * dot(gproj, kl_ref[pl.ds(pl.multiple_of(i * step_rows, block), step_rows), :], 1, 1)
        ig_ref[:, cols] = back.astype(BF16)

    out_ref[...] = acc[...].astype(BF16)


def shards(
    hidden_in, out_grad, base_levels, base_scales, kron_outer, kron_left, kron_right,
    sparse_rows, sparse_cols, sparse_count, sparse_values,
):
    tile_rows, tile_cols = base_levels.shape
    slots, block = sparse_values.shape[2], sparse_values.shape[3]
    own = hidden_in.shape[0]
    pad = -own % 16
    rank = kron_left.shape[1]
    row_blocks, col_blocks = tile_rows // block, tile_cols // block
    n_s = lax.axis_size("dp") * lax.axis_size("sub")
    n_t = lax.axis_size("tp")
    tokens = own * n_s
    rows, cols = sparse_rows[0, 0], sparse_cols[0, 0]
    live = jnp.arange(slots) < sparse_count[0, 0]
    hit = ((rows * col_blocks + cols)[:, None] == jnp.arange(row_blocks * col_blocks)[None]) & live[:, None]
    slot_map = slots + jnp.sum(jnp.where(hit, jnp.arange(slots)[:, None] - slots, 0), axis=0)

    x = lax.all_gather(jnp.pad(hidden_in, ((0, pad), (0, 0))), ("dp", "sub"), axis=0, tiled=True)
    dy = lax.all_gather(jnp.pad(out_grad, ((0, pad), (0, 0))), "tp", axis=0, tiled=True)
    full = x.shape[0]
    step_rows = pick_rows(tile_rows, tile_cols, block, tile_rows // base_scales.shape[0])
    vmem = pl.BlockSpec(memory_space=pltpu.VMEM)
    smem = pl.BlockSpec(memory_space=pltpu.SMEM)
    out, ig, go, gl, gr, gs = pl.pallas_call(
        functools.partial(kernel, tokens, step_rows),
        in_specs=[smem] * 5 + [vmem] * 6 + [pl.BlockSpec(memory_space=pl.ANY)],
        out_specs=[vmem] * 6,
        out_shape=[
            jax.ShapeDtypeStruct((full, tile_cols), BF16),
            jax.ShapeDtypeStruct((full, tile_rows), BF16),
            jax.ShapeDtypeStruct((1, 1), F32),
            jax.ShapeDtypeStruct((rank, tile_rows), F32),
            jax.ShapeDtypeStruct((rank, tile_cols), F32),
            jax.ShapeDtypeStruct((slots, block, block), F32),
        ],
        scratch_shapes=[
            pltpu.VMEM((2, step_rows, tile_cols), BF16),
            pltpu.VMEM((step_rows, tile_cols), BF16),
            pltpu.VMEM((full, tile_cols), F32),
            pltpu.VMEM(base_scales.shape, F32),
            pltpu.VMEM((slots + 1, block, block), BF16),
            pltpu.SemaphoreType.DMA((2,)),
        ],
        compiler_params=pltpu.CompilerParams(vmem_limit_bytes=50 << 20),
    )(
        slot_map, rows, cols, sparse_count, kron_outer, x, dy, kron_left, kron_right,
        base_scales, sparse_values[0, 0], base_levels,
    )
    layer_out = lax.psum_scatter(out, "tp", scatter_dimension=0, tiled=True)[:own]
    input_grad = lax.psum_scatter(ig, ("dp", "sub"), scatter_dimension=0, tiled=True)[:own]
    gl, gr = lax.optimization_barrier(lax.psum(jnp.concatenate([gl, gr], 1), ("tp", "dp", "sub"))), None
    gl, gr = gl[:, :tile_rows], gl[:, tile_rows:]
    return layer_out, input_grad, go, gl.T, gr, gs[None, None]


def solution(mesh):
    return jax.shard_map(
        shards,
        mesh=mesh,
        in_specs=(
            P(("grp", "dp", "sub"), "tp"),
            P(("grp", "tp"), ("dp", "sub")),
            P("tp", ("dp", "sub")),
            P("tp", ("dp", "sub")),
            P("tp", ("dp", "sub")),
            P(),
            P(),
            P("tp", ("dp", "sub"), None),
            P("tp", ("dp", "sub"), None),
            P("tp", ("dp", "sub")),
            P("tp", ("dp", "sub"), None, None, None),
        ),
        out_specs=(
            P(("grp", "tp"), ("dp", "sub")),
            P(("grp", "dp", "sub"), "tp"),
            P(("grp", "tp"), ("dp", "sub")),
            P("grp", None),
            P("grp", None),
            P(("grp", "tp"), ("dp", "sub"), None, None, None),
        ),
        check_vma=False,
    )
```

```python
import functools

import jax
import jax.numpy as jnp
from jax import lax
from jax.experimental import pallas as pl
from jax.experimental.pallas import tpu as pltpu
from jax.sharding import PartitionSpec as P

F32 = jnp.float32
BF16 = jnp.bfloat16


def dot(a, b, ca, cb):
    return lax.dot_general(a, b, (((ca,), (cb,)), ((), ())), preferred_element_type=F32)


def pick_rows(tile_rows, tile_cols, block, quant):
    blocks = tile_rows // block
    best = tile_rows
    for n in range(1, blocks):
        if blocks % n == 0 and n * block * tile_cols <= 1 << 20 and n * block % (8 * quant) == 0:
            best = n * block
    return tile_rows if tile_rows * tile_cols <= 1 << 20 else best


def kernel(
    tokens, step_rows,
    slot_ref, rows_ref, cols_ref, count_ref, coef_ref,
    x_ref, dy_ref, kl_ref, kr_ref, sc_ref, val_ref, w_hbm,
    out_ref, ig_ref, go_ref, g_ref, gs_ref,
    wbuf, wdq, acc, scf, vals, wsem,
):
    tile_rows, tile_cols = w_hbm.shape
    slots, block = val_ref.shape[0], val_ref.shape[1]
    col_blocks = tile_cols // block
    step_blocks = step_rows // block
    steps = tile_rows // step_rows
    quant = tile_rows // sc_ref.shape[0]
    inv = 1.0 / tokens
    coef = coef_ref[0, 0]

    def fetch(i, slot):
        return pltpu.make_async_copy(
            w_hbm.at[pl.ds(i * step_rows, step_rows)], wbuf.at[slot], wsem.at[slot]
        )

    fetch(0, 0).start()
    scf[...] = sc_ref[...].astype(F32)
    vals[pl.ds(0, slots)] = val_ref[...]
    vals[slots] = jnp.zeros((block, block), BF16)

    proj = dot(x_ref[...], kl_ref[...], 1, 1).astype(BF16)
    gproj = dot(dy_ref[...], kr_ref[...], 1, 1).astype(BF16)
    go_ref[...] = (jnp.sum(proj.astype(F32) * gproj.astype(F32)) * inv).reshape(1, 1)
    g_ref[...] = jnp.zeros_like(g_ref)
    g_ref[:, :tile_rows] = (dot(gproj, x_ref[...], 0, 0) * (coef * inv)).astype(BF16)
    g_ref[:, tile_rows:tile_rows + tile_cols] = (dot(proj, dy_ref[...], 0, 0) * (coef * inv)).astype(BF16)
    acc[...] = coef * dot(proj, kr_ref[...], 1, 0)

    @pl.loop(0, slots)
    def _(m):
        xr = x_ref[:, pl.ds(pl.multiple_of(rows_ref[m] * block, block), block)]
        dc = dy_ref[:, pl.ds(pl.multiple_of(cols_ref[m] * block, block), block)]
        live = jnp.where(m < count_ref[0, 0], inv, 0.0)
        gs_ref[m] = dot(xr, dc, 0, 0) * live

    @pl.loop(0, steps)
    def _(i):
        slot = lax.rem(i, 2)

        @pl.when(i + 1 < steps)
        def _():
            fetch(i + 1, 1 - slot).start()

        fetch(i, slot).wait()
        groups = step_rows // quant
        if steps == 1:
            scales = scf[...]
        else:
            scales = scf[pl.ds(pl.multiple_of(i * groups, 8), groups), :]
        for rb in range(step_blocks):
            for cb in range(col_blocks):
                delta = vals[slot_ref[(i * step_blocks + rb) * col_blocks + cb]]
                for q in range(block // quant):
                    r0 = rb * block + q * quant
                    lv = wbuf[slot, r0:r0 + quant, cb * block:(cb + 1) * block]
                    s = scales[r0 // quant:r0 // quant + 1, cb * block:(cb + 1) * block]
                    s16 = jnp.broadcast_to(s, (16, block)).astype(BF16)
                    w = lv.reshape(quant // 16, 16, block) * s16[None]
                    w = w.reshape(quant, block) + delta[q * quant:(q + 1) * quant]
                    wdq[r0:r0 + quant, cb * block:(cb + 1) * block] = w
        cols = pl.ds(pl.multiple_of(i * step_rows, block), step_rows)
        acc[...] += dot(x_ref[:, cols], wdq[...], 1, 0)
        back = dot(dy_ref[...], wdq[...], 1, 1)
        back += coef * dot(gproj, kl_ref[:, cols], 1, 0)
        ig_ref[:, cols] = back.astype(BF16)

    out_ref[...] = acc[...].astype(BF16)


def places():
    sizes = [lax.axis_size(a) for a in ("dp", "sub", "tp")]
    return sizes, [lax.axis_index(a) for a in ("dp", "sub", "tp")]


def target(dp, sub, tp):
    return {"dp": dp, "sub": sub, "tp": tp}


def remote(src, dst, send, recv, index, where):
    return pltpu.make_async_remote_copy(
        src_ref=src, dst_ref=dst, send_sem=send.at[index], recv_sem=recv.at[index],
        device_id=where, device_id_type=pl.DeviceIdType.MESH,
    )


def greet(peers):
    barrier = pltpu.get_barrier_semaphore()
    for peer in peers:
        pl.semaphore_signal(barrier, inc=1, device_id=peer, device_id_type=pl.DeviceIdType.MESH)
    pl.semaphore_wait(barrier, len(peers))


def pieces(width):
    n = next(c for c in (4, 2, 1) if width % (128 * c) == 0)
    return [(c * (width // n), width // n) for c in range(n)]


def gather_kernel(h_ref, d_ref, x_ref, dy_ref, local, dps, dpr, subs, subr, fws, fwr, tps, tpr):
    (n_dp, n_sub, n_t), (dp, sub, tp) = places()
    cuts = pieces(h_ref.shape[1])
    dp_peers = [target(lax.rem(dp + a, n_dp), sub, tp) for a in range(1, n_dp)]
    sub_peers = [target(dp, lax.rem(sub + b, n_sub), tp) for b in range(1, n_sub)]
    tp_peers = [target(dp, sub, lax.rem(tp + c, n_t)) for c in range(1, n_t)]
    greet(dp_peers + sub_peers + tp_peers)
    me = dp * n_sub + sub
    by_dp, copies = [], []
    for i, (lo, size) in enumerate(cuts):
        for a, peer in enumerate(dp_peers):
            c = remote(h_ref.at[:, pl.ds(lo, size)], x_ref.at[me, :, pl.ds(lo, size)], dps, dpr, i * len(dp_peers) + a, peer)
            c.start()
            by_dp.append(c)
    for t, peer in enumerate(tp_peers):
        copies.append(remote(d_ref, dy_ref.at[tp], tps, tpr, t, peer))
    for b, peer in enumerate(sub_peers):
        copies.append(remote(h_ref, x_ref.at[me], subs, subr, b, peer))
    for c in copies:
        c.start()
    mine = [
        pltpu.make_async_copy(h_ref, x_ref.at[me], local.at[0]),
        pltpu.make_async_copy(d_ref, dy_ref.at[tp], local.at[1]),
    ]
    for c in mine:
        c.start()
    forwards = []
    for i, (lo, size) in enumerate(cuts):
        for a in range(len(dp_peers)):
            k = i * len(dp_peers) + a
            by_dp[k].wait_recv()
            came = lax.rem(dp + n_dp - 1 - a, n_dp) * n_sub + sub
            view = x_ref.at[came, :, pl.ds(lo, size)]
            for b, peer in enumerate(sub_peers):
                c = remote(view, view, fws, fwr, k * len(sub_peers) + b, peer)
                c.start()
                forwards.append(c)
    for c in by_dp:
        c.wait_send()
    for c in copies + forwards + mine:
        c.wait()


def gather(h, d):
    (n_dp, n_sub, n_t), _ = places()
    hbm = pl.BlockSpec(memory_space=pl.ANY)
    dma = pltpu.SemaphoreType.DMA
    n = len(pieces(h.shape[1])) * (n_dp - 1)
    return pl.pallas_call(
        gather_kernel,
        in_specs=[hbm] * 2,
        out_specs=[hbm] * 2,
        out_shape=[
            jax.ShapeDtypeStruct((n_dp * n_sub,) + h.shape, BF16),
            jax.ShapeDtypeStruct((n_t,) + d.shape, BF16),
        ],
        scratch_shapes=[
            dma((2,)), dma((n,)), dma((n,)), dma((n_sub - 1,)), dma((n_sub - 1,)),
            dma((n * (n_sub - 1),)), dma((n * (n_sub - 1),)), dma((n_t - 1,)), dma((n_t - 1,)),
        ],
        compiler_params=pltpu.CompilerParams(collective_id=0, has_side_effects=True),
    )(h, d)


def reduce_kernel(
    ig_ref, out_ref, g_ref, lo_ref, igo_ref, gsum_ref,
    sub_buf, sum_buf, dp_buf, tp_buf, g1_buf, g_mine, g2_buf, g_all,
    s_sub, r_sub, s_dp, r_dp, s_tp, r_tp, s_g1, r_g1, s_g2, r_g2, s_g3, r_g3,
):
    (n_dp, n_sub, n_t), (dp, sub, tp) = places()
    own = lo_ref.shape[0]
    ws = g_mine.shape[1]
    cuts = pieces(ig_ref.shape[3])
    dp_ids = [lax.rem(dp + a, n_dp) for a in range(n_dp)]
    sub_ids = [lax.rem(sub + b, n_sub) for b in range(n_sub)]
    near = [(a, b) for a in range(n_dp) for b in range(n_sub) if a or b]
    near_peers = [target(dp_ids[a], sub_ids[b], tp) for a, b in near]
    tp_peers = [target(dp, sub, lax.rem(tp + c, n_t)) for c in range(1, n_t)]
    greet(near_peers + tp_peers)

    def part(j):
        return pl.ds(pl.multiple_of(j * ws, 128), ws)

    me = dp * n_sub + sub
    g1 = [
        remote(g_ref.at[:, part(dp_ids[a] * n_sub + sub_ids[b])], g1_buf.at[k], s_g1, r_g1, k, near_peers[k])
        for k, (a, b) in enumerate(near)
    ]
    for c in g1:
        c.start()
    by_sub = []
    for i, (lo, size) in enumerate(cuts):
        for b in range(1, n_sub):
            c = remote(
                ig_ref.at[:, sub_ids[b], :, pl.ds(lo, size)], sub_buf.at[b - 1, :, :, pl.ds(lo, size)],
                s_sub, r_sub, i * (n_sub - 1) + b - 1, target(dp, sub_ids[b], tp),
            )
            c.start()
            by_sub.append(c)
    by_tp = [
        remote(out_ref.at[lax.rem(tp + t + 1, n_t)], tp_buf.at[t], s_tp, r_tp, t, peer)
        for t, peer in enumerate(tp_peers)
    ]
    for c in by_tp:
        c.start()

    def pair(d, lo, size):
        total = ig_ref[d, sub, :, lo:lo + size].astype(F32)
        for b in range(n_sub - 1):
            total += sub_buf[b, d, :, lo:lo + size].astype(F32)
        return total

    by_dp = []

    def forward(i):
        lo, size = cuts[i]
        for b in range(n_sub - 1):
            by_sub[i * (n_sub - 1) + b].wait_recv()
        for a in range(1, n_dp):
            sum_buf[a - 1, :, lo:lo + size] = pair(dp_ids[a], lo, size).astype(BF16)
            c = remote(
                sum_buf.at[a - 1, :, pl.ds(lo, size)], dp_buf.at[a - 1, :, pl.ds(lo, size)],
                s_dp, r_dp, i * (n_dp - 1) + a - 1, target(dp_ids[a], sub, tp),
            )
            c.start()
            by_dp.append(c)

    forward(0)
    for c in g1:
        c.wait_recv()
    total = g_ref[:, part(me)].astype(F32)
    for k in range(len(near)):
        total += g1_buf[k].astype(F32)
    g_mine[...] = total.astype(BF16)
    g2 = [remote(g_mine, g2_buf.at[tp], s_g2, r_g2, t, peer) for t, peer in enumerate(tp_peers)]
    for c in g2:
        c.start()
    g2_buf[tp] = total.astype(BF16)
    for i in range(1, len(cuts)):
        forward(i)

    for c in g2:
        c.wait_recv()
    total = g2_buf[0].astype(F32)
    for t in range(1, n_t):
        total += g2_buf[t].astype(F32)
    g_all[:, part(me)] = total.astype(BF16)
    g3 = [
        remote(g_all.at[:, part(me)], g_all.at[:, part(me)], s_g3, r_g3, k, near_peers[k])
        for k in range(len(near))
    ]
    for c in g3:
        c.start()

    for c in by_tp:
        c.wait_recv()
    total = out_ref[tp].astype(F32)
    for t in range(n_t - 1):
        total += tp_buf[t].astype(F32)
    lo_ref[...] = total[:own].astype(BF16)

    for i, (lo, size) in enumerate(cuts):
        total = pair(dp, lo, size)
        for a in range(n_dp - 1):
            by_dp[i * (n_dp - 1) + a].wait_recv()
            total += dp_buf[a, :, lo:lo + size].astype(F32)
        igo_ref[:, lo:lo + size] = total[:own].astype(BF16)

    for c in g3:
        c.wait_recv()
    gsum_ref[...] = g_all[...].astype(F32)
    for c in g1 + by_sub + by_tp + by_dp + g2 + g3:
        c.wait_send()


def reduce(ig, out, g, own):
    (n_dp, n_sub, n_t), _ = places()
    padded, tile_rows = ig.shape[2:]
    tile_cols = out.shape[2]
    rank, wide = g.shape
    n_s = n_dp * n_sub
    ws = wide // n_s
    cuts = len(pieces(tile_rows))
    vmem = pl.BlockSpec(memory_space=pltpu.VMEM)
    counts = [cuts * (n_sub - 1), cuts * (n_dp - 1), n_t - 1, n_s - 1, n_t - 1, n_s - 1]
    return pl.pallas_call(
        reduce_kernel,
        in_specs=[vmem] * 3,
        out_specs=[vmem] * 3,
        out_shape=[
            jax.ShapeDtypeStruct((own, tile_cols), BF16),
            jax.ShapeDtypeStruct((own, tile_rows), BF16),
            jax.ShapeDtypeStruct((rank, wide), F32),
        ],
        scratch_shapes=[
            pltpu.VMEM((n_sub - 1, n_dp, padded, tile_rows), BF16),
            pltpu.VMEM((n_dp - 1, padded, tile_rows), BF16),
            pltpu.VMEM((n_dp - 1, padded, tile_rows), BF16),
            pltpu.VMEM((n_t - 1, padded, tile_cols), BF16),
            pltpu.VMEM((n_s - 1, rank, ws), BF16),
            pltpu.VMEM((rank, ws), BF16),
            pltpu.VMEM((n_t, rank, ws), BF16),
            pltpu.VMEM((rank, wide), BF16),
        ] + [pltpu.SemaphoreType.DMA((n,)) for n in counts for _ in range(2)],
        compiler_params=pltpu.CompilerParams(
            collective_id=1, has_side_effects=True, vmem_limit_bytes=40 << 20
        ),
    )(ig, out, g)


def shards(
    hidden_in, out_grad, base_levels, base_scales, kron_outer, kron_left, kron_right,
    sparse_rows, sparse_cols, sparse_count, sparse_values,
):
    tile_rows, tile_cols = base_levels.shape
    slots, block = sparse_values.shape[2], sparse_values.shape[3]
    own = hidden_in.shape[0]
    pad = -own % 16
    rank = kron_left.shape[1]
    row_blocks, col_blocks = tile_rows // block, tile_cols // block
    n_s = lax.axis_size("dp") * lax.axis_size("sub")
    n_t = lax.axis_size("tp")
    tokens = own * n_s
    rows, cols = sparse_rows[0, 0], sparse_cols[0, 0]
    live = jnp.arange(slots) < sparse_count[0, 0]
    hit = ((rows * col_blocks + cols)[:, None] == jnp.arange(row_blocks * col_blocks)[None]) & live[:, None]
    slot_map = slots + jnp.sum(jnp.where(hit, jnp.arange(slots)[:, None] - slots, 0), axis=0)

    x, dy = gather(jnp.pad(hidden_in, ((0, pad), (0, 0))), jnp.pad(out_grad, ((0, pad), (0, 0))))
    x = x.reshape(-1, tile_rows)
    dy = dy.reshape(-1, tile_cols)
    unit = 128 * n_s
    wide = -(-(tile_rows + tile_cols) // unit) * unit
    full = x.shape[0]
    step_rows = pick_rows(tile_rows, tile_cols, block, tile_rows // base_scales.shape[0])
    vmem = pl.BlockSpec(memory_space=pltpu.VMEM)
    smem = pl.BlockSpec(memory_space=pltpu.SMEM)
    out, ig, go, g, gs = pl.pallas_call(
        functools.partial(kernel, tokens, step_rows),
        in_specs=[smem] * 5 + [vmem] * 6 + [pl.BlockSpec(memory_space=pl.ANY)],
        out_specs=[vmem] * 5,
        out_shape=[
            jax.ShapeDtypeStruct((full, tile_cols), BF16),
            jax.ShapeDtypeStruct((full, tile_rows), BF16),
            jax.ShapeDtypeStruct((1, 1), F32),
            jax.ShapeDtypeStruct((rank, wide), BF16),
            jax.ShapeDtypeStruct((slots, block, block), F32),
        ],
        scratch_shapes=[
            pltpu.VMEM((2, step_rows, tile_cols), BF16),
            pltpu.VMEM((step_rows, tile_cols), BF16),
            pltpu.VMEM((full, tile_cols), F32),
            pltpu.VMEM(base_scales.shape, F32),
            pltpu.VMEM((slots + 1, block, block), BF16),
            pltpu.SemaphoreType.DMA((2,)),
        ],
        compiler_params=pltpu.CompilerParams(vmem_limit_bytes=50 << 20),
    )(
        slot_map, rows, cols, sparse_count, kron_outer, x, dy, kron_left.T, kron_right,
        base_scales, sparse_values[0, 0], base_levels,
    )
    layer_out, input_grad, g = reduce(
        ig.reshape(lax.axis_size("dp"), lax.axis_size("sub"), own + pad, tile_rows),
        out.reshape(n_t, own + pad, tile_cols), g, own,
    )
    gl, gr = g[:, :tile_rows], g[:, tile_rows:tile_rows + tile_cols]
    return layer_out, input_grad, go, gl.T, gr, gs[None, None]


def solution(mesh):
    return jax.shard_map(
        shards,
        mesh=mesh,
        in_specs=(
            P(("grp", "dp", "sub"), "tp"),
            P(("grp", "tp"), ("dp", "sub")),
            P("tp", ("dp", "sub")),
            P("tp", ("dp", "sub")),
            P("tp", ("dp", "sub")),
            P(),
            P(),
            P("tp", ("dp", "sub"), None),
            P("tp", ("dp", "sub"), None),
            P("tp", ("dp", "sub")),
            P("tp", ("dp", "sub"), None, None, None),
        ),
        out_specs=(
            P(("grp", "tp"), ("dp", "sub")),
            P(("grp", "dp", "sub"), "tp"),
            P(("grp", "tp"), ("dp", "sub")),
            P("grp", None),
            P("grp", None),
            P(("grp", "tp"), ("dp", "sub"), None, None, None),
        ),
        check_vma=False,
    )
```

```python
import functools

import jax
import jax.numpy as jnp
from jax import lax
from jax.experimental import pallas as pl
from jax.experimental.pallas import tpu as pltpu
from jax.sharding import PartitionSpec as P

F32 = jnp.float32
BF16 = jnp.bfloat16


def dot(a, b, ca, cb):
    return lax.dot_general(a, b, (((ca,), (cb,)), ((), ())), preferred_element_type=F32)


def pick_rows(tile_rows, tile_cols, block, quant):
    blocks = tile_rows // block
    best = tile_rows
    for n in range(1, blocks):
        if blocks % n == 0 and n * block * tile_cols <= 1 << 20 and n * block % (8 * quant) == 0:
            best = n * block
    return tile_rows if tile_rows * tile_cols <= 1 << 20 else best


def kernel(
    tokens, step_rows,
    slot_ref, rows_ref, cols_ref, count_ref, coef_ref,
    xin_ref, dyin_ref, kl_ref, kr_ref, sc_ref, val_ref, w_hbm,
    out_ref, ig_ref, go_ref, g_ref, gs_ref,
    wbuf, wdq, acc, scf, vals, x_ref, dy_ref, wsem,
):
    tile_rows, tile_cols = w_hbm.shape
    slots, block = val_ref.shape[0], val_ref.shape[1]
    col_blocks = tile_cols // block
    step_blocks = step_rows // block
    steps = tile_rows // step_rows
    quant = tile_rows // sc_ref.shape[0]
    inv = 1.0 / tokens
    coef = coef_ref[0, 0]

    def fetch(i, slot):
        return pltpu.make_async_copy(
            w_hbm.at[pl.ds(i * step_rows, step_rows)], wbuf.at[slot], wsem.at[slot]
        )

    fetch(0, 0).start()
    for src, dst in ((xin_ref, x_ref), (dyin_ref, dy_ref)):
        parts, own, _ = src.shape
        each = dst.shape[0] // parts
        dst[...] = jnp.zeros_like(dst)
        for j in range(parts):
            dst[j * each:j * each + own, :] = src[j]
    scf[...] = sc_ref[...].astype(F32)
    vals[pl.ds(0, slots)] = val_ref[...]
    vals[slots] = jnp.zeros((block, block), BF16)

    proj = dot(x_ref[...], kl_ref[...], 1, 1).astype(BF16)
    gproj = dot(dy_ref[...], kr_ref[...], 1, 1).astype(BF16)
    go_ref[...] = (jnp.sum(proj.astype(F32) * gproj.astype(F32)) * inv).reshape(1, 1)
    g_ref[...] = jnp.zeros_like(g_ref)
    g_ref[:, :tile_rows] = (dot(gproj, x_ref[...], 0, 0) * (coef * inv)).astype(BF16)
    g_ref[:, tile_rows:tile_rows + tile_cols] = (dot(proj, dy_ref[...], 0, 0) * (coef * inv)).astype(BF16)
    acc[...] = coef * dot(proj, kr_ref[...], 1, 0)

    @pl.loop(0, slots)
    def _(m):
        xr = x_ref[:, pl.ds(pl.multiple_of(rows_ref[m] * block, block), block)]
        dc = dy_ref[:, pl.ds(pl.multiple_of(cols_ref[m] * block, block), block)]
        live = jnp.where(m < count_ref[0, 0], inv, 0.0)
        gs_ref[m] = dot(xr, dc, 0, 0) * live

    @pl.loop(0, steps)
    def _(i):
        slot = lax.rem(i, 2)

        @pl.when(i + 1 < steps)
        def _():
            fetch(i + 1, 1 - slot).start()

        fetch(i, slot).wait()
        groups = step_rows // quant
        if steps == 1:
            scales = scf[...]
        else:
            scales = scf[pl.ds(pl.multiple_of(i * groups, 8), groups), :]
        for rb in range(step_blocks):
            for cb in range(col_blocks):
                delta = vals[slot_ref[(i * step_blocks + rb) * col_blocks + cb]]
                for q in range(block // quant):
                    r0 = rb * block + q * quant
                    lv = wbuf[slot, r0:r0 + quant, cb * block:(cb + 1) * block]
                    s = scales[r0 // quant:r0 // quant + 1, cb * block:(cb + 1) * block]
                    s16 = jnp.broadcast_to(s, (16, block)).astype(BF16)
                    w = lv.reshape(quant // 16, 16, block) * s16[None]
                    w = w.reshape(quant, block) + delta[q * quant:(q + 1) * quant]
                    wdq[r0:r0 + quant, cb * block:(cb + 1) * block] = w
        cols = pl.ds(pl.multiple_of(i * step_rows, block), step_rows)
        acc[...] += dot(x_ref[:, cols], wdq[...], 1, 0)
        back = dot(dy_ref[...], wdq[...], 1, 1)
        back += coef * dot(gproj, kl_ref[:, cols], 1, 0)
        ig_ref[:, cols] = back.astype(BF16)

    out_ref[...] = acc[...].astype(BF16)


def places():
    sizes = [lax.axis_size(a) for a in ("dp", "sub", "tp")]
    return sizes, [lax.axis_index(a) for a in ("dp", "sub", "tp")]


def target(dp, sub, tp):
    return {"dp": dp, "sub": sub, "tp": tp}


def remote(src, dst, send, recv, index, where):
    return pltpu.make_async_remote_copy(
        src_ref=src, dst_ref=dst, send_sem=send.at[index], recv_sem=recv.at[index],
        device_id=where, device_id_type=pl.DeviceIdType.MESH,
    )


def greet(peers):
    barrier = pltpu.get_barrier_semaphore()
    for peer in peers:
        pl.semaphore_signal(barrier, inc=1, device_id=peer, device_id_type=pl.DeviceIdType.MESH)
    pl.semaphore_wait(barrier, len(peers))


def pieces(width):
    n = next(c for c in (4, 2, 1) if width % (128 * c) == 0)
    return [(c * (width // n), width // n) for c in range(n)]


def gather_kernel(h_ref, d_ref, x_ref, dy_ref, dps, dpr, subs, subr, fws, fwr, tps, tpr):
    (n_dp, n_sub, n_t), (dp, sub, tp) = places()
    cuts = pieces(h_ref.shape[1])
    dp_peers = [target(lax.rem(dp + a, n_dp), sub, tp) for a in range(1, n_dp)]
    sub_peers = [target(dp, lax.rem(sub + b, n_sub), tp) for b in range(1, n_sub)]
    tp_peers = [target(dp, sub, lax.rem(tp + c, n_t)) for c in range(1, n_t)]
    greet(dp_peers + sub_peers + tp_peers)
    me = dp * n_sub + sub
    by_dp, copies = [], []
    for i, (lo, size) in enumerate(cuts):
        for a, peer in enumerate(dp_peers):
            c = remote(h_ref.at[:, pl.ds(lo, size)], x_ref.at[me, :, pl.ds(lo, size)], dps, dpr, i * len(dp_peers) + a, peer)
            c.start()
            by_dp.append(c)
    for t, peer in enumerate(tp_peers):
        copies.append(remote(d_ref, dy_ref.at[tp], tps, tpr, t, peer))
    for b, peer in enumerate(sub_peers):
        copies.append(remote(h_ref, x_ref.at[me], subs, subr, b, peer))
    for c in copies:
        c.start()
    x_ref[me] = h_ref[...]
    dy_ref[tp] = d_ref[...]
    forwards = []
    for i, (lo, size) in enumerate(cuts):
        for a in range(len(dp_peers)):
            k = i * len(dp_peers) + a
            by_dp[k].wait_recv()
            came = lax.rem(dp + n_dp - 1 - a, n_dp) * n_sub + sub
            view = x_ref.at[came, :, pl.ds(lo, size)]
            for b, peer in enumerate(sub_peers):
                c = remote(view, view, fws, fwr, k * len(sub_peers) + b, peer)
                c.start()
                forwards.append(c)
    for c in by_dp:
        c.wait_send()
    for c in copies + forwards:
        c.wait()


def gather(h, d):
    (n_dp, n_sub, n_t), _ = places()
    vmem = pl.BlockSpec(memory_space=pltpu.VMEM)
    dma = pltpu.SemaphoreType.DMA
    n = len(pieces(h.shape[1])) * (n_dp - 1)
    return pl.pallas_call(
        gather_kernel,
        in_specs=[vmem] * 2,
        out_specs=[vmem] * 2,
        out_shape=[
            jax.ShapeDtypeStruct((n_dp * n_sub,) + h.shape, BF16),
            jax.ShapeDtypeStruct((n_t,) + d.shape, BF16),
        ],
        scratch_shapes=[
            dma((n,)), dma((n,)), dma((n_sub - 1,)), dma((n_sub - 1,)),
            dma((n * (n_sub - 1),)), dma((n * (n_sub - 1),)), dma((n_t - 1,)), dma((n_t - 1,)),
        ],
        compiler_params=pltpu.CompilerParams(
            collective_id=0, has_side_effects=True, vmem_limit_bytes=8 << 20
        ),
    )(h, d)


def reduce_kernel(
    ig_ref, out_ref, g_ref, lo_ref, igo_ref, gsum_ref,
    sub_buf, sum_buf, dp_buf, tp_buf, g1_buf, g_mine, g2_buf, g_all,
    s_sub, r_sub, s_dp, r_dp, s_tp, r_tp, s_g1, r_g1, s_g2, r_g2, s_g3, r_g3,
):
    (n_dp, n_sub, n_t), (dp, sub, tp) = places()
    own = lo_ref.shape[0]
    ws = g_mine.shape[1]
    cuts = pieces(ig_ref.shape[3])
    dp_ids = [lax.rem(dp + a, n_dp) for a in range(n_dp)]
    sub_ids = [lax.rem(sub + b, n_sub) for b in range(n_sub)]
    near = [(a, b) for a in range(n_dp) for b in range(n_sub) if a or b]
    near_peers = [target(dp_ids[a], sub_ids[b], tp) for a, b in near]
    tp_peers = [target(dp, sub, lax.rem(tp + c, n_t)) for c in range(1, n_t)]
    greet(near_peers + tp_peers)

    def part(j):
        return pl.ds(pl.multiple_of(j * ws, 128), ws)

    me = dp * n_sub + sub
    g1 = [
        remote(g_ref.at[:, part(dp_ids[a] * n_sub + sub_ids[b])], g1_buf.at[k], s_g1, r_g1, k, near_peers[k])
        for k, (a, b) in enumerate(near)
    ]
    for c in g1:
        c.start()
    by_sub = []
    for i, (lo, size) in enumerate(cuts):
        for b in range(1, n_sub):
            c = remote(
                ig_ref.at[:, sub_ids[b], :, pl.ds(lo, size)], sub_buf.at[b - 1, :, :, pl.ds(lo, size)],
                s_sub, r_sub, i * (n_sub - 1) + b - 1, target(dp, sub_ids[b], tp),
            )
            c.start()
            by_sub.append(c)
    by_tp = [
        remote(out_ref.at[lax.rem(tp + t + 1, n_t)], tp_buf.at[t], s_tp, r_tp, t, peer)
        for t, peer in enumerate(tp_peers)
    ]
    for c in by_tp:
        c.start()

    def pair(d, lo, size):
        total = ig_ref[d, sub, :, lo:lo + size].astype(F32)
        for b in range(n_sub - 1):
            total += sub_buf[b, d, :, lo:lo + size].astype(F32)
        return total

    by_dp = []

    def forward(i):
        lo, size = cuts[i]
        for b in range(n_sub - 1):
            by_sub[i * (n_sub - 1) + b].wait_recv()
        for a in range(1, n_dp):
            sum_buf[a - 1, :, lo:lo + size] = pair(dp_ids[a], lo, size).astype(BF16)
            c = remote(
                sum_buf.at[a - 1, :, pl.ds(lo, size)], dp_buf.at[a - 1, :, pl.ds(lo, size)],
                s_dp, r_dp, i * (n_dp - 1) + a - 1, target(dp_ids[a], sub, tp),
            )
            c.start()
            by_dp.append(c)

    forward(0)
    for c in g1:
        c.wait_recv()
    total = g_ref[:, part(me)].astype(F32)
    for k in range(len(near)):
        total += g1_buf[k].astype(F32)
    g_mine[...] = total.astype(BF16)
    g2 = [remote(g_mine, g2_buf.at[tp], s_g2, r_g2, t, peer) for t, peer in enumerate(tp_peers)]
    for c in g2:
        c.start()
    g2_buf[tp] = total.astype(BF16)
    for i in range(1, len(cuts)):
        forward(i)

    for c in g2:
        c.wait_recv()
    total = g2_buf[0].astype(F32)
    for t in range(1, n_t):
        total += g2_buf[t].astype(F32)
    g_all[:, part(me)] = total.astype(BF16)
    g3 = [
        remote(g_all.at[:, part(me)], g_all.at[:, part(me)], s_g3, r_g3, k, near_peers[k])
        for k in range(len(near))
    ]
    for c in g3:
        c.start()

    for c in by_tp:
        c.wait_recv()
    total = out_ref[tp].astype(F32)
    for t in range(n_t - 1):
        total += tp_buf[t].astype(F32)
    lo_ref[...] = total[:own].astype(BF16)

    for i, (lo, size) in enumerate(cuts):
        total = pair(dp, lo, size)
        for a in range(n_dp - 1):
            by_dp[i * (n_dp - 1) + a].wait_recv()
            total += dp_buf[a, :, lo:lo + size].astype(F32)
        igo_ref[:, lo:lo + size] = total[:own].astype(BF16)

    for c in g3:
        c.wait_recv()
    gsum_ref[...] = g_all[...].astype(F32)
    for c in g1 + by_sub + by_tp + by_dp + g2 + g3:
        c.wait_send()


def reduce(ig, out, g, own):
    (n_dp, n_sub, n_t), _ = places()
    padded, tile_rows = ig.shape[2:]
    tile_cols = out.shape[2]
    rank, wide = g.shape
    n_s = n_dp * n_sub
    ws = wide // n_s
    cuts = len(pieces(tile_rows))
    vmem = pl.BlockSpec(memory_space=pltpu.VMEM)
    counts = [cuts * (n_sub - 1), cuts * (n_dp - 1), n_t - 1, n_s - 1, n_t - 1, n_s - 1]
    return pl.pallas_call(
        reduce_kernel,
        in_specs=[vmem] * 3,
        out_specs=[vmem] * 3,
        out_shape=[
            jax.ShapeDtypeStruct((own, tile_cols), BF16),
            jax.ShapeDtypeStruct((own, tile_rows), BF16),
            jax.ShapeDtypeStruct((rank, wide), F32),
        ],
        scratch_shapes=[
            pltpu.VMEM((n_sub - 1, n_dp, padded, tile_rows), BF16),
            pltpu.VMEM((n_dp - 1, padded, tile_rows), BF16),
            pltpu.VMEM((n_dp - 1, padded, tile_rows), BF16),
            pltpu.VMEM((n_t - 1, padded, tile_cols), BF16),
            pltpu.VMEM((n_s - 1, rank, ws), BF16),
            pltpu.VMEM((rank, ws), BF16),
            pltpu.VMEM((n_t, rank, ws), BF16),
            pltpu.VMEM((rank, wide), BF16),
        ] + [pltpu.SemaphoreType.DMA((n,)) for n in counts for _ in range(2)],
        compiler_params=pltpu.CompilerParams(
            collective_id=1, has_side_effects=True, vmem_limit_bytes=40 << 20
        ),
    )(ig, out, g)


def shards(
    hidden_in, out_grad, base_levels, base_scales, kron_outer, kron_left, kron_right,
    sparse_rows, sparse_cols, sparse_count, sparse_values,
):
    tile_rows, tile_cols = base_levels.shape
    slots, block = sparse_values.shape[2], sparse_values.shape[3]
    own = hidden_in.shape[0]
    pad = -own % 16
    rank = kron_left.shape[1]
    row_blocks, col_blocks = tile_rows // block, tile_cols // block
    n_s = lax.axis_size("dp") * lax.axis_size("sub")
    n_t = lax.axis_size("tp")
    tokens = own * n_s
    rows, cols = sparse_rows[0, 0], sparse_cols[0, 0]
    live = jnp.arange(slots) < sparse_count[0, 0]
    hit = ((rows * col_blocks + cols)[:, None] == jnp.arange(row_blocks * col_blocks)[None]) & live[:, None]
    slot_map = slots + jnp.sum(jnp.where(hit, jnp.arange(slots)[:, None] - slots, 0), axis=0)

    x, dy = gather(hidden_in, out_grad)
    unit = 128 * n_s
    wide = -(-(tile_rows + tile_cols) // unit) * unit
    full = n_s * (own + pad)
    step_rows = pick_rows(tile_rows, tile_cols, block, tile_rows // base_scales.shape[0])
    vmem = pl.BlockSpec(memory_space=pltpu.VMEM)
    smem = pl.BlockSpec(memory_space=pltpu.SMEM)
    out, ig, go, g, gs = pl.pallas_call(
        functools.partial(kernel, tokens, step_rows),
        in_specs=[smem] * 5 + [vmem] * 6 + [pl.BlockSpec(memory_space=pl.ANY)],
        out_specs=[vmem] * 5,
        out_shape=[
            jax.ShapeDtypeStruct((full, tile_cols), BF16),
            jax.ShapeDtypeStruct((full, tile_rows), BF16),
            jax.ShapeDtypeStruct((1, 1), F32),
            jax.ShapeDtypeStruct((rank, wide), BF16),
            jax.ShapeDtypeStruct((slots, block, block), F32),
        ],
        scratch_shapes=[
            pltpu.VMEM((2, step_rows, tile_cols), BF16),
            pltpu.VMEM((step_rows, tile_cols), BF16),
            pltpu.VMEM((full, tile_cols), F32),
            pltpu.VMEM(base_scales.shape, F32),
            pltpu.VMEM((slots + 1, block, block), BF16),
            pltpu.VMEM((full, tile_rows), BF16),
            pltpu.VMEM((n_t * (own + pad), tile_cols), BF16),
            pltpu.SemaphoreType.DMA((2,)),
        ],
        compiler_params=pltpu.CompilerParams(vmem_limit_bytes=50 << 20),
    )(
        slot_map, rows, cols, sparse_count, kron_outer, x, dy, kron_left.T, kron_right,
        base_scales, sparse_values[0, 0], base_levels,
    )
    layer_out, input_grad, g = reduce(
        ig.reshape(lax.axis_size("dp"), lax.axis_size("sub"), own + pad, tile_rows),
        out.reshape(n_t, own + pad, tile_cols), g, own,
    )
    gl, gr = g[:, :tile_rows], g[:, tile_rows:tile_rows + tile_cols]
    return layer_out, input_grad, go, gl.T, gr, gs[None, None]


def solution(mesh):
    return jax.shard_map(
        shards,
        mesh=mesh,
        in_specs=(
            P(("grp", "dp", "sub"), "tp"),
            P(("grp", "tp"), ("dp", "sub")),
            P("tp", ("dp", "sub")),
            P("tp", ("dp", "sub")),
            P("tp", ("dp", "sub")),
            P(),
            P(),
            P("tp", ("dp", "sub"), None),
            P("tp", ("dp", "sub"), None),
            P("tp", ("dp", "sub")),
            P("tp", ("dp", "sub"), None, None, None),
        ),
        out_specs=(
            P(("grp", "tp"), ("dp", "sub")),
            P(("grp", "dp", "sub"), "tp"),
            P(("grp", "tp"), ("dp", "sub")),
            P("grp", None),
            P("grp", None),
            P(("grp", "tp"), ("dp", "sub"), None, None, None),
        ),
        check_vma=False,
    )
```

```python
import functools

import jax
import jax.numpy as jnp
from jax import lax
from jax.experimental import pallas as pl
from jax.experimental.pallas import tpu as pltpu
from jax.sharding import PartitionSpec as P

F32 = jnp.float32
BF16 = jnp.bfloat16


def dot(a, b, ca, cb):
    return lax.dot_general(a, b, (((ca,), (cb,)), ((), ())), preferred_element_type=F32)


def pick_rows(tile_rows, tile_cols, block, quant):
    blocks = tile_rows // block
    best = tile_rows
    for n in range(1, blocks):
        if blocks % n == 0 and n * block * tile_cols <= 1 << 20 and n * block % (8 * quant) == 0:
            best = n * block
    return tile_rows if tile_rows * tile_cols <= 1 << 20 else best


def kernel(
    tokens, step_rows,
    slot_ref, rows_ref, cols_ref, count_ref, coef_ref,
    xin_ref, dyin_ref, kl_ref, kr_ref, sc_ref, val_ref, w_hbm,
    out_ref, ig_ref, go_ref, g_ref, gs_ref,
    wbuf, wdq, acc, scf, vals, x_ref, dy_ref, wsem,
):
    tile_rows, tile_cols = w_hbm.shape
    slots, block = val_ref.shape[0], val_ref.shape[1]
    col_blocks = tile_cols // block
    step_blocks = step_rows // block
    steps = tile_rows // step_rows
    quant = tile_rows // sc_ref.shape[0]
    inv = 1.0 / tokens
    coef = coef_ref[0, 0]

    def fetch(i, slot):
        return pltpu.make_async_copy(
            w_hbm.at[pl.ds(i * step_rows, step_rows)], wbuf.at[slot], wsem.at[slot]
        )

    fetch(0, 0).start()
    for src, dst in ((xin_ref, x_ref), (dyin_ref, dy_ref)):
        parts, own, _ = src.shape
        each = dst.shape[0] // parts
        dst[...] = jnp.zeros_like(dst)
        for j in range(parts):
            dst[j * each:j * each + own, :] = src[j]
    scf[...] = sc_ref[...].astype(F32)
    vals[pl.ds(0, slots)] = val_ref[...]
    vals[slots] = jnp.zeros((block, block), BF16)

    proj = dot(x_ref[...], kl_ref[...], 1, 1).astype(BF16)
    gproj = dot(dy_ref[...], kr_ref[...], 1, 1).astype(BF16)
    go_ref[...] = (jnp.sum(proj.astype(F32) * gproj.astype(F32)) * inv).reshape(1, 1)
    g_ref[...] = jnp.zeros_like(g_ref)
    g_ref[:, :tile_rows] = (dot(gproj, x_ref[...], 0, 0) * (coef * inv)).astype(BF16)
    g_ref[:, tile_rows:tile_rows + tile_cols] = (dot(proj, dy_ref[...], 0, 0) * (coef * inv)).astype(BF16)
    acc[...] = coef * dot(proj, kr_ref[...], 1, 0)

    @pl.loop(0, slots)
    def _(m):
        xr = x_ref[:, pl.ds(pl.multiple_of(rows_ref[m] * block, block), block)]
        dc = dy_ref[:, pl.ds(pl.multiple_of(cols_ref[m] * block, block), block)]
        live = jnp.where(m < count_ref[0, 0], inv, 0.0)
        gs_ref[m] = dot(xr, dc, 0, 0) * live

    @pl.loop(0, steps)
    def _(i):
        slot = lax.rem(i, 2)

        @pl.when(i + 1 < steps)
        def _():
            fetch(i + 1, 1 - slot).start()

        fetch(i, slot).wait()
        groups = step_rows // quant
        if steps == 1:
            scales = scf[...]
        else:
            scales = scf[pl.ds(pl.multiple_of(i * groups, 8), groups), :]
        for rb in range(step_blocks):
            for cb in range(col_blocks):
                delta = vals[slot_ref[(i * step_blocks + rb) * col_blocks + cb]]
                for q in range(block // quant):
                    r0 = rb * block + q * quant
                    lv = wbuf[slot, r0:r0 + quant, cb * block:(cb + 1) * block]
                    s = scales[r0 // quant:r0 // quant + 1, cb * block:(cb + 1) * block]
                    s16 = jnp.broadcast_to(s, (16, block)).astype(BF16)
                    w = lv.reshape(quant // 16, 16, block) * s16[None]
                    w = w.reshape(quant, block) + delta[q * quant:(q + 1) * quant]
                    wdq[r0:r0 + quant, cb * block:(cb + 1) * block] = w
        cols = pl.ds(pl.multiple_of(i * step_rows, block), step_rows)
        acc[...] += dot(x_ref[:, cols], wdq[...], 1, 0)
        back = dot(dy_ref[...], wdq[...], 1, 1)
        back += coef * dot(gproj, kl_ref[:, cols], 1, 0)
        ig_ref[:, cols] = back.astype(BF16)

    out_ref[...] = acc[...].astype(BF16)


def places():
    sizes = [lax.axis_size(a) for a in ("dp", "sub", "tp")]
    return sizes, [lax.axis_index(a) for a in ("dp", "sub", "tp")]


def target(dp, sub, tp):
    return {"dp": dp, "sub": sub, "tp": tp}


def remote(src, dst, send, recv, index, where):
    return pltpu.make_async_remote_copy(
        src_ref=src, dst_ref=dst, send_sem=send.at[index], recv_sem=recv.at[index],
        device_id=where, device_id_type=pl.DeviceIdType.MESH,
    )


def greet(peers):
    barrier = pltpu.get_barrier_semaphore()
    for peer in peers:
        pl.semaphore_signal(barrier, inc=1, device_id=peer, device_id_type=pl.DeviceIdType.MESH)
    pl.semaphore_wait(barrier, len(peers))


def pieces(width):
    n = next(c for c in (4, 2, 1) if width % (128 * c) == 0)
    return [(c * (width // n), width // n) for c in range(n)]


def gather_kernel(h_ref, d_ref, x_ref, dy_ref, dps, dpr, subs, subr, fws, fwr, tps, tpr):
    (n_dp, n_sub, n_t), (dp, sub, tp) = places()
    cuts = pieces(h_ref.shape[1])
    dp_peers = [target(lax.rem(dp + a, n_dp), sub, tp) for a in range(1, n_dp)]
    sub_peers = [target(dp, lax.rem(sub + b, n_sub), tp) for b in range(1, n_sub)]
    tp_peers = [target(dp, sub, lax.rem(tp + c, n_t)) for c in range(1, n_t)]
    greet(dp_peers + sub_peers + tp_peers)
    me = dp * n_sub + sub
    by_dp, copies = [], []
    for i, (lo, size) in enumerate(cuts):
        for a, peer in enumerate(dp_peers):
            c = remote(h_ref.at[:, pl.ds(lo, size)], x_ref.at[me, :, pl.ds(lo, size)], dps, dpr, i * len(dp_peers) + a, peer)
            c.start()
            by_dp.append(c)
    for t, peer in enumerate(tp_peers):
        copies.append(remote(d_ref, dy_ref.at[tp], tps, tpr, t, peer))
    for b, peer in enumerate(sub_peers):
        copies.append(remote(h_ref, x_ref.at[me], subs, subr, b, peer))
    for c in copies:
        c.start()
    x_ref[me] = h_ref[...]
    dy_ref[tp] = d_ref[...]
    forwards = []
    for i, (lo, size) in enumerate(cuts):
        for a in range(len(dp_peers)):
            k = i * len(dp_peers) + a
            by_dp[k].wait_recv()
            came = lax.rem(dp + n_dp - 1 - a, n_dp) * n_sub + sub
            view = x_ref.at[came, :, pl.ds(lo, size)]
            for b, peer in enumerate(sub_peers):
                c = remote(view, view, fws, fwr, k * len(sub_peers) + b, peer)
                c.start()
                forwards.append(c)
    for c in by_dp:
        c.wait_send()
    for c in copies + forwards:
        c.wait()


def gather(h, d):
    (n_dp, n_sub, n_t), _ = places()
    vmem = pl.BlockSpec(memory_space=pltpu.VMEM)
    dma = pltpu.SemaphoreType.DMA
    n = len(pieces(h.shape[1])) * (n_dp - 1)
    return pl.pallas_call(
        gather_kernel,
        in_specs=[vmem] * 2,
        out_specs=[vmem] * 2,
        out_shape=[
            jax.ShapeDtypeStruct((n_dp * n_sub,) + h.shape, BF16),
            jax.ShapeDtypeStruct((n_t,) + d.shape, BF16),
        ],
        scratch_shapes=[
            dma((n,)), dma((n,)), dma((n_sub - 1,)), dma((n_sub - 1,)),
            dma((n * (n_sub - 1),)), dma((n * (n_sub - 1),)), dma((n_t - 1,)), dma((n_t - 1,)),
        ],
        compiler_params=pltpu.CompilerParams(
            collective_id=0, has_side_effects=True, vmem_limit_bytes=8 << 20
        ),
    )(h, d)


def reduce_kernel(
    ig_ref, out_ref, g_ref, lo_ref, igo_ref, gsum_ref,
    sub_buf, sum_buf, dp_buf, tp_buf, g1_buf, g_mine, g2_buf, g_all,
    s_sub, r_sub, s_dp, r_dp, s_tp, r_tp, s_g1, r_g1, s_g2, r_g2, s_g3, r_g3,
):
    (n_dp, n_sub, n_t), (dp, sub, tp) = places()
    own = lo_ref.shape[0]
    ws = g_mine.shape[1]
    cuts = pieces(ig_ref.shape[3])
    dp_ids = [lax.rem(dp + a, n_dp) for a in range(n_dp)]
    sub_ids = [lax.rem(sub + b, n_sub) for b in range(n_sub)]
    near = [(a, b) for a in range(n_dp) for b in range(n_sub) if a or b]
    near_peers = [target(dp_ids[a], sub_ids[b], tp) for a, b in near]
    tp_peers = [target(dp, sub, lax.rem(tp + c, n_t)) for c in range(1, n_t)]
    greet(near_peers + tp_peers)

    def part(j):
        return pl.ds(pl.multiple_of(j * ws, 128), ws)

    me = dp * n_sub + sub
    g1 = [
        remote(g_ref.at[:, part(dp_ids[a] * n_sub + sub_ids[b])], g1_buf.at[k], s_g1, r_g1, k, near_peers[k])
        for k, (a, b) in enumerate(near)
    ]
    for c in g1:
        c.start()
    by_sub = []
    for i, (lo, size) in enumerate(cuts):
        for b in range(1, n_sub):
            c = remote(
                ig_ref.at[:, sub_ids[b], :, pl.ds(lo, size)], sub_buf.at[b - 1, :, :, pl.ds(lo, size)],
                s_sub, r_sub, i * (n_sub - 1) + b - 1, target(dp, sub_ids[b], tp),
            )
            c.start()
            by_sub.append(c)
    by_tp = [
        remote(out_ref.at[lax.rem(tp + t + 1, n_t)], tp_buf.at[t], s_tp, r_tp, t, peer)
        for t, peer in enumerate(tp_peers)
    ]
    for c in by_tp:
        c.start()

    def pair(d, lo, size):
        total = ig_ref[d, sub, :, lo:lo + size].astype(F32)
        for b in range(n_sub - 1):
            total += sub_buf[b, d, :, lo:lo + size].astype(F32)
        return total

    by_dp = []

    def forward(i):
        lo, size = cuts[i]
        for b in range(n_sub - 1):
            by_sub[i * (n_sub - 1) + b].wait_recv()
        for a in range(1, n_dp):
            sum_buf[a - 1, :, lo:lo + size] = pair(dp_ids[a], lo, size).astype(BF16)
            c = remote(
                sum_buf.at[a - 1, :, pl.ds(lo, size)], dp_buf.at[a - 1, :, pl.ds(lo, size)],
                s_dp, r_dp, i * (n_dp - 1) + a - 1, target(dp_ids[a], sub, tp),
            )
            c.start()
            by_dp.append(c)

    forward(0)
    for c in g1:
        c.wait_recv()
    total = g_ref[:, part(me)].astype(F32)
    for k in range(len(near)):
        total += g1_buf[k].astype(F32)
    g_mine[...] = total.astype(BF16)
    g2 = [remote(g_mine, g2_buf.at[tp], s_g2, r_g2, t, peer) for t, peer in enumerate(tp_peers)]
    for c in g2:
        c.start()
    g2_buf[tp] = total.astype(BF16)
    for i in range(1, len(cuts)):
        forward(i)

    for c in g2:
        c.wait_recv()
    total = g2_buf[0].astype(F32)
    for t in range(1, n_t):
        total += g2_buf[t].astype(F32)
    g_all[:, part(me)] = total.astype(BF16)
    g3 = [
        remote(g_all.at[:, part(me)], g_all.at[:, part(me)], s_g3, r_g3, k, near_peers[k])
        for k in range(len(near))
    ]
    for c in g3:
        c.start()

    for c in by_tp:
        c.wait_recv()
    total = out_ref[tp].astype(F32)
    for t in range(n_t - 1):
        total += tp_buf[t].astype(F32)
    lo_ref[...] = total[:own].astype(BF16)

    for i, (lo, size) in enumerate(cuts):
        total = pair(dp, lo, size)
        for a in range(n_dp - 1):
            by_dp[i * (n_dp - 1) + a].wait_recv()
            total += dp_buf[a, :, lo:lo + size].astype(F32)
        igo_ref[:, lo:lo + size] = total[:own].astype(BF16)

    for c in g3:
        c.wait_recv()
    gsum_ref[...] = g_all[...].astype(F32)
    for c in g1 + by_sub + by_tp + by_dp + g2 + g3:
        c.wait_send()


def reduce(ig, out, g, own):
    (n_dp, n_sub, n_t), _ = places()
    padded, tile_rows = ig.shape[2:]
    tile_cols = out.shape[2]
    rank, wide = g.shape
    n_s = n_dp * n_sub
    ws = wide // n_s
    cuts = len(pieces(tile_rows))
    vmem = pl.BlockSpec(memory_space=pltpu.VMEM)
    counts = [cuts * (n_sub - 1), cuts * (n_dp - 1), n_t - 1, n_s - 1, n_t - 1, n_s - 1]
    return pl.pallas_call(
        reduce_kernel,
        in_specs=[vmem] * 3,
        out_specs=[vmem] * 3,
        out_shape=[
            jax.ShapeDtypeStruct((own, tile_cols), BF16),
            jax.ShapeDtypeStruct((own, tile_rows), BF16),
            jax.ShapeDtypeStruct((rank, wide), F32),
        ],
        scratch_shapes=[
            pltpu.VMEM((n_sub - 1, n_dp, padded, tile_rows), BF16),
            pltpu.VMEM((n_dp - 1, padded, tile_rows), BF16),
            pltpu.VMEM((n_dp - 1, padded, tile_rows), BF16),
            pltpu.VMEM((n_t - 1, padded, tile_cols), BF16),
            pltpu.VMEM((n_s - 1, rank, ws), BF16),
            pltpu.VMEM((rank, ws), BF16),
            pltpu.VMEM((n_t, rank, ws), BF16),
            pltpu.VMEM((rank, wide), BF16),
        ] + [pltpu.SemaphoreType.DMA((n,)) for n in counts for _ in range(2)],
        compiler_params=pltpu.CompilerParams(
            collective_id=1, has_side_effects=True, vmem_limit_bytes=16 << 20
        ),
    )(ig, out, g)


def shards(
    hidden_in, out_grad, base_levels, base_scales, kron_outer, kron_left, kron_right,
    sparse_rows, sparse_cols, sparse_count, sparse_values,
):
    tile_rows, tile_cols = base_levels.shape
    slots, block = sparse_values.shape[2], sparse_values.shape[3]
    own = hidden_in.shape[0]
    pad = -own % 16
    rank = kron_left.shape[1]
    row_blocks, col_blocks = tile_rows // block, tile_cols // block
    n_s = lax.axis_size("dp") * lax.axis_size("sub")
    n_t = lax.axis_size("tp")
    tokens = own * n_s
    rows, cols = sparse_rows[0, 0], sparse_cols[0, 0]
    live = jnp.arange(slots) < sparse_count[0, 0]
    hit = ((rows * col_blocks + cols)[:, None] == jnp.arange(row_blocks * col_blocks)[None]) & live[:, None]
    slot_map = slots + jnp.sum(jnp.where(hit, jnp.arange(slots)[:, None] - slots, 0), axis=0)

    x, dy = gather(hidden_in, out_grad)
    unit = 128 * n_s
    wide = -(-(tile_rows + tile_cols) // unit) * unit
    full = n_s * (own + pad)
    step_rows = pick_rows(tile_rows, tile_cols, block, tile_rows // base_scales.shape[0])
    vmem = pl.BlockSpec(memory_space=pltpu.VMEM)
    smem = pl.BlockSpec(memory_space=pltpu.SMEM)
    out, ig, go, g, gs = pl.pallas_call(
        functools.partial(kernel, tokens, step_rows),
        in_specs=[smem] * 5 + [vmem] * 6 + [pl.BlockSpec(memory_space=pl.ANY)],
        out_specs=[vmem] * 5,
        out_shape=[
            jax.ShapeDtypeStruct((full, tile_cols), BF16),
            jax.ShapeDtypeStruct((full, tile_rows), BF16),
            jax.ShapeDtypeStruct((1, 1), F32),
            jax.ShapeDtypeStruct((rank, wide), BF16),
            jax.ShapeDtypeStruct((slots, block, block), F32),
        ],
        scratch_shapes=[
            pltpu.VMEM((2, step_rows, tile_cols), BF16),
            pltpu.VMEM((step_rows, tile_cols), BF16),
            pltpu.VMEM((full, tile_cols), F32),
            pltpu.VMEM(base_scales.shape, F32),
            pltpu.VMEM((slots + 1, block, block), BF16),
            pltpu.VMEM((full, tile_rows), BF16),
            pltpu.VMEM((n_t * (own + pad), tile_cols), BF16),
            pltpu.SemaphoreType.DMA((2,)),
        ],
        compiler_params=pltpu.CompilerParams(vmem_limit_bytes=24 << 20),
    )(
        slot_map, rows, cols, sparse_count, kron_outer, x, dy, kron_left.T, kron_right,
        base_scales, sparse_values[0, 0], base_levels,
    )
    layer_out, input_grad, g = reduce(
        ig.reshape(lax.axis_size("dp"), lax.axis_size("sub"), own + pad, tile_rows),
        out.reshape(n_t, own + pad, tile_cols), g, own,
    )
    gl, gr = g[:, :tile_rows], g[:, tile_rows:tile_rows + tile_cols]
    return layer_out, input_grad, go, gl.T, gr, gs[None, None]


def solution(mesh):
    return jax.shard_map(
        shards,
        mesh=mesh,
        in_specs=(
            P(("grp", "dp", "sub"), "tp"),
            P(("grp", "tp"), ("dp", "sub")),
            P("tp", ("dp", "sub")),
            P("tp", ("dp", "sub")),
            P("tp", ("dp", "sub")),
            P(),
            P(),
            P("tp", ("dp", "sub"), None),
            P("tp", ("dp", "sub"), None),
            P("tp", ("dp", "sub")),
            P("tp", ("dp", "sub"), None, None, None),
        ),
        out_specs=(
            P(("grp", "tp"), ("dp", "sub")),
            P(("grp", "dp", "sub"), "tp"),
            P(("grp", "tp"), ("dp", "sub")),
            P("grp", None),
            P("grp", None),
            P(("grp", "tp"), ("dp", "sub"), None, None, None),
        ),
        check_vma=False,
    )
```
